32 devices in a mesh: groups: 2 (over x), shard: 16 (over z, y, core).
Axes of the slice: x: 2, y: 2, z: 4, core: 2. Of those that a mesh axis runs over, the one named last changes fastest.
Arguments:
- features: bfloat16 [8192, 4096], P(('groups', 'shard')), parts along dimension 0, may hold values from -6 to 6
- cotangent: bfloat16 [8192, 4096], P(('groups', 'shard')), parts along dimension 0, may hold values from -0.029907227 to 0.029907227
- member_weight: bfloat16 [1024, 4096], P('shard'), may hold values from -0.1875 to 0.1875
- shared_weight: bfloat16 [256, 2048], P('shard'), may hold values from -0.375 to 0.375
- shared_coords: int32 [8, 2], replicated, may hold values from 0 to 15, as said below
Outputs:
- activated: bfloat16 [8192, 4096], P(('groups', 'shard')), parts along dimension 0
- member_grad: float32 [2048, 4096], P(('groups', 'shard')), parts along dimension 0
- shared_grad: float32 [512, 2048], P(('groups', 'shard')), parts along dimension 0
The draws below stay inside these ranges and needn't reach their ends.
There are 2 independent parts, one for each index of `groups`. The reference program is written for one: setup_inputs(seed, part) draws one part's arguments, and reference() takes and returns one part's arrays. A program takes and returns all parts, laid end to end along the dimension named above; an argument that names none is the same for every part. Nothing has to cross between parts.
Inputs may be any that keep to these rules, and one draw needn't show every extreme that they name: `shared_coords`: the 8 pairs (row block, column block) are distinct, and none lies in a member's diagonal square: row block // 4 differs from column block // 4.
All inputs are finite; a program needn't handle non-finite values.
Results may differ from the reference program's by a relative error of at most 0.0029.
Values may be sent and summed in bfloat16 or wider, within the bound.
A program may use at most 128 MiB of HBM per device.

```python
import jax
import jax.numpy as jnp
from jax import lax

MW = 1024
MEMBERS = 4
B = 256
NSH = 8
F = 4096
TOKENS = 4096


def draw_shared_coords(key, part):
    grid = MEMBERS * MW // B
    per_member = MW // B
    cells = jnp.arange(grid * grid, dtype=jnp.int32)
    row_ids = cells // grid
    col_ids = cells % grid
    inside = row_ids // per_member == col_ids // per_member
    scores = jax.random.randint(key, (grid * grid,), 0, 1 << 20, dtype=jnp.int32) * (grid * grid) + cells
    scores = scores + inside.astype(jnp.int32) * (1 << 29)
    order = jnp.argsort(scores)
    chosen = order[:NSH].astype(jnp.int32)
    return jnp.stack([chosen // grid, chosen % grid], axis=1).astype(jnp.int32)


def raised(result, stream_key, source, target, blocks, factor):
    def block_of(axis_at):
        return (jnp.arange(result.shape[axis_at]) // (result.shape[axis_at] // blocks)).reshape((-1,) + (1,) * (result.ndim - 1 - axis_at))

    one_side = jax.random.permutation(stream_key, blocks)[block_of(target)]
    other_side = (block_of(target) + blocks // 2) % blocks
    return jnp.where((block_of(source) == one_side) | (block_of(source) == other_side), factor * result, result)


def block_levels(own_key, shape, cuts, smallest, top_value):
    def one(axis_at, parts):
        steps = jax.random.uniform(jax.random.fold_in(jax.random.fold_in(own_key, 6), axis_at), (parts,), jnp.float32, smallest / len(cuts), top_value / len(cuts))
        return jnp.repeat(jnp.exp(steps), shape[axis_at] // parts).reshape((-1,) + (1,) * (len(shape) - axis_at - 1))

    factor_of = one(*cuts[0])
    for cut in cuts[1:]:
        factor_of = factor_of * one(*cut)
    return factor_of


def centred(stream_key, shape, scale, reach, cuts=(), held_as=jnp.bfloat16):
    loudness = block_levels(stream_key, shape, cuts, -0.22, 0.18) if cuts else 1.0
    entries = jax.random.normal(stream_key, shape, jnp.float32) * scale * loudness
    return jnp.minimum(jnp.maximum(entries, -reach), reach).astype(held_as)


def noise_with(stream_key, shape, spread, bound, cuts, heavy, kind=jnp.bfloat16):
    entries = spread * jax.random.normal(stream_key, shape, jnp.float32)
    if cuts:
        entries = entries * block_levels(stream_key, shape, cuts, -0.22, 0.18)
    return jnp.clip(raised(entries, jax.random.fold_in(stream_key, 3), *heavy), -bound, bound).astype(kind)


def setup_inputs(seed: int = 0, part: int = 0) -> dict:
    key_of = jax.random.split(jax.random.key(seed), 6)
    part_splits = jax.random.split(jax.random.fold_in(key_of[5], part), 6)
    features = noise_with(part_splits[0], (TOKENS, F), 1.0, 6.0, ((0, 16),), (0, 1, 16, 2.0))
    cotangent = centred(part_splits[1], (TOKENS, F), 0.005, 0.029907227, ((0, 16),))
    member_weight = centred(key_of[2], (MW, F), MW ** -0.5, 0.1875, ((0, 16),))
    shared_weight = centred(key_of[3], (B, NSH * B), B ** -0.5, 0.375, ((0, 16),))
    shared_coords = draw_shared_coords(jax.random.fold_in(key_of[5], 71), part)
    return dict(features=features, cotangent=cotangent, member_weight=member_weight, shared_weight=shared_weight, shared_coords=shared_coords)


ROOT_HALF = 0.7071067811865476
INV_ROOT_TWO_PI = 0.3989422804014327


def gelu_slope(hidden):
    return 0.5 * (1.0 + jax.scipy.special.erf(hidden * ROOT_HALF)) + hidden * INV_ROOT_TWO_PI * jnp.exp(-0.5 * hidden * hidden)


def reference(features, cotangent, member_weight, shared_weight, shared_coords):
    token_rows = features.shape[0]
    width = features.shape[1]
    members = width // MW
    x_members = features.astype(jnp.float32).reshape(token_rows, members, MW)
    w_members = member_weight.astype(jnp.float32).reshape(MW, members, MW)
    hidden = jnp.einsum("tmi,imj->tmj", x_members, w_members, precision=lax.Precision.HIGHEST).reshape(token_rows, width)
    for index in range(NSH):
        row_start = shared_coords[index, 0].astype(jnp.int32) * B
        col_start = shared_coords[index, 1].astype(jnp.int32) * B
        inputs = lax.dynamic_slice_in_dim(features, row_start, B, 1)
        weight = shared_weight[:, index * B:(index + 1) * B]
        current = lax.dynamic_slice_in_dim(hidden, col_start, B, 1)
        added = current + jnp.dot(inputs, weight, preferred_element_type=jnp.float32)
        hidden = lax.dynamic_update_slice_in_dim(hidden, added, col_start, 1)
    activated = jax.nn.gelu(hidden, approximate=False).astype(jnp.bfloat16)
    grad_hidden = (cotangent.astype(jnp.float32) * gelu_slope(hidden)).astype(jnp.bfloat16)
    grad_members = grad_hidden.astype(jnp.float32).reshape(token_rows, members, MW)
    member_grad = jnp.einsum("tmi,tmj->imj", x_members, grad_members, precision=lax.Precision.HIGHEST).reshape(MW, width)
    pieces = []
    for index in range(NSH):
        row_start = shared_coords[index, 0].astype(jnp.int32) * B
        col_start = shared_coords[index, 1].astype(jnp.int32) * B
        inputs = lax.dynamic_slice_in_dim(features, row_start, B, 1)
        grad_block = lax.dynamic_slice_in_dim(grad_hidden, col_start, B, 1)
        pieces.append(jnp.dot(inputs.T, grad_block, preferred_element_type=jnp.float32))
    shared_grad = jnp.stack(pieces, axis=1).reshape(B, NSH * B)
    return activated, member_grad, shared_grad
```

```python
import functools

import jax
import jax.numpy as jnp
from jax import lax
from jax.experimental import pallas as pl
from jax.experimental.pallas import tpu as pltpu
from jax.sharding import PartitionSpec as P

ROOT_HALF = 0.7071067811865476
INV_ROOT_TWO_PI = 0.3989422804014327
MESH = pl.DeviceIdType.MESH
VMEM_BYTES = 56 * 2**20


def reversed_bits(value, bits):
    out = 0
    for b in range(bits):
        out = out + ((value // 2**b) % 2) * 2 ** (bits - 1 - b)
    return out


def flipped(value, b):
    return value + (1 - 2 * ((value // 2**b) % 2)) * 2**b


def greet(me, bits):
    barrier = pltpu.get_barrier_semaphore()
    for b in range(bits):
        pl.semaphore_signal(
            barrier, inc=1, device_id={"shard": flipped(me, b)}, device_id_type=MESH
        )
    pl.semaphore_wait(barrier, bits)


def gather_kernel(bits, chunks, chunk, member_ref, folded_ref, out_ref, send, recv, local):
    me = lax.axis_index("shard")
    pos = reversed_bits(me, bits)
    greet(me, bits)

    def own(c):
        if c == chunks - 1:
            return folded_ref
        return member_ref.at[:, c * chunk : (c + 1) * chunk]

    def copy(c, k):
        if k == 0:
            src, dst = own(c), out_ref.at[c, pos]
        else:
            src = dst = out_ref.at[c, pl.ds((pos // 2**k) * 2**k, 2**k)]
        return pltpu.make_async_remote_copy(
            src_ref=src,
            dst_ref=dst,
            send_sem=send.at[c, k],
            recv_sem=recv.at[c, k],
            device_id={"shard": flipped(me, bits - 1 - k)},
            device_id_type=MESH,
        )

    def local_copy(c):
        return pltpu.make_async_copy(own(c), out_ref.at[c, pos], local.at[c])

    for wave in range(chunks + bits):
        for k in range(bits + 1):
            c = wave - k
            if c < 0 or c >= chunks:
                continue
            if k == 0:
                local_copy(c).start()
            if k == 1:
                local_copy(c).wait()
            if k > 0:
                copy(c, k - 1).wait_recv()
            if k < bits:
                copy(c, k).start()
    for c in range(chunks):
        for k in range(bits):
            copy(c, k).wait_send()


def layer_kernel(
    bits, block, coords_ref, feat_ref, feat_m_ref, cot_ref, w_ref, s_ref,
    act_ref, term_ref, sterm_ref, hid_ref,
):
    step = pl.program_id(0)
    count = 2**bits
    rows = w_ref.shape[2]
    chunk = w_ref.shape[3]
    shared_count = s_ref.shape[0]
    per = chunk // block
    weights = jnp.concatenate(
        [w_ref[0, reversed_bits(d, bits)] for d in range(count)], axis=0
    )
    hid_ref[...] = jnp.dot(feat_m_ref[...], weights, preferred_element_type=jnp.float32)

    def shared_inputs(s):
        start = pl.multiple_of(coords_ref[s, 0] * block, block)
        return feat_ref[:, pl.ds(start, block)]

    for s in range(shared_count):
        for part in range(per):
            @pl.when(coords_ref[s, 1] == step * per + part)
            def _():
                cols = slice(part * block, (part + 1) * block)
                hid_ref[:, cols] += jnp.dot(
                    shared_inputs(s), s_ref[s], preferred_element_type=jnp.float32
                )

    hidden = hid_ref[...]
    phi = 0.5 * (1.0 + lax.erf(hidden * ROOT_HALF))
    act_ref[...] = (hidden * phi).astype(act_ref.dtype)
    slope = phi + hidden * INV_ROOT_TWO_PI * jnp.exp(-0.5 * hidden * hidden)
    grad = (cot_ref[...].astype(jnp.float32) * slope).astype(jnp.bfloat16)
    term = lax.dot_general(
        feat_m_ref[...], grad, (((0,), (0,)), ((), ())), preferred_element_type=jnp.float32
    )
    for d in range(count):
        term_ref[0, reversed_bits(d, bits)] = term[d * rows : (d + 1) * rows]
    for s in range(shared_count):
        for part in range(per):
            @pl.when(coords_ref[s, 1] == step * per + part)
            def _():
                sterm_ref[s] = lax.dot_general(
                    shared_inputs(s),
                    grad[:, part * block : (part + 1) * block],
                    (((0,), (0,)), ((), ())),
                    preferred_element_type=jnp.float32,
                )


def scatter_kernel(
    bits, chunks, chunk, term_ref, folded_ref, member_out, folded_out, acc, out_buf, in_buf,
    send, recv, local,
):
    me = lax.axis_index("shard")
    pos = reversed_bits(me, bits)
    count = 2**bits

    def load(c):
        src = folded_ref if c == chunks - 1 else term_ref.at[c]
        return pltpu.make_async_copy(src, acc.at[c], local.at[c])

    for c in range(chunks):
        load(c).start()
    greet(me, bits)

    def span(k):
        size = count // 2 ** (k + 1)
        return count - count // 2**k, size

    def copy(c, k):
        first, size = span(k)
        return pltpu.make_async_remote_copy(
            src_ref=out_buf.at[c, pl.ds(first, size)],
            dst_ref=in_buf.at[c, pl.ds(first, size)],
            send_sem=send.at[c, k],
            recv_sem=recv.at[c, k],
            device_id={"shard": flipped(me, k)},
            device_id_type=MESH,
        )

    for wave in range(chunks + bits):
        for k in range(bits + 1):
            c = wave - k
            if c < 0 or c >= chunks:
                continue
            if k == 0:
                load(c).wait()
            else:
                copy(c, k - 1).wait_recv()
                first, size = span(k - 1)
                kept = (pos // size) * size

                @pl.loop(0, size)
                def _(i):
                    acc[c, kept + i] += in_buf[c, first + i].astype(jnp.float32)

            if k < bits:
                first, size = span(k)
                leaving = (flipped(pos, bits - 1 - k) // size) * size

                @pl.loop(0, size)
                def _(i):
                    out_buf[c, first + i] = acc[c, leaving + i].astype(out_buf.dtype)

                copy(c, k).start()
            elif c == chunks - 1:
                folded_out[...] = acc[c, pos]
            else:
                member_out[:, c * chunk : (c + 1) * chunk] = acc[c, pos]
    for c in range(chunks):
        for k in range(bits):
            copy(c, k).wait_send()


def per_device(features, cotangent, member_weight, shared_weight, shared_coords):
    count = lax.axis_size("shard")
    bits = count.bit_length() - 1
    tokens, width = features.shape
    rows = member_weight.shape[0]
    member_width = rows * count
    local = shared_weight.shape[0]
    block = local * count
    shared_count = shared_coords.shape[0]
    ratio = member_width // block
    chunk = shared_count * block // ratio
    member_chunks = width // chunk
    chunks = member_chunks + 1
    per = chunk // block
    f32 = jnp.float32
    any_space = pl.BlockSpec(memory_space=pl.ANY)
    vmem_space = pl.BlockSpec(memory_space=pltpu.VMEM)

    folded = jnp.transpose(shared_weight.reshape(local, ratio, chunk), (1, 0, 2)).reshape(rows, chunk)
    gathered = pl.pallas_call(
        functools.partial(gather_kernel, bits, chunks, chunk),
        out_shape=jax.ShapeDtypeStruct((chunks, count, rows, chunk), jnp.bfloat16),
        in_specs=[any_space, any_space],
        out_specs=any_space,
        scratch_shapes=[
            pltpu.SemaphoreType.DMA((chunks, bits)),
            pltpu.SemaphoreType.DMA((chunks, bits)),
            pltpu.SemaphoreType.DMA((chunks,)),
        ],
        compiler_params=pltpu.CompilerParams(collective_id=0, has_side_effects=True),
        name="gather_weights",
    )(member_weight, folded)

    order = [reversed_bits(d, bits) for d in range(count)]
    twos = (2,) * bits
    back = tuple(reversed(range(bits)))
    shared_pieces = gathered[member_chunks].reshape(twos + (ratio, local, per, block))
    shared_blocks = jnp.transpose(
        shared_pieces, (bits, bits + 2) + back + (bits + 1, bits + 3)
    ).reshape(shared_count, block, block)

    member_chunk_count = member_width // chunk
    activated, term, shared_term = pl.pallas_call(
        functools.partial(layer_kernel, bits, block),
        grid_spec=pltpu.PrefetchScalarGridSpec(
            num_scalar_prefetch=1,
            grid=(member_chunks,),
            in_specs=[
                pl.BlockSpec((tokens, width), lambda j, coords: (0, 0)),
                pl.BlockSpec((tokens, member_width), lambda j, coords: (0, j // member_chunk_count)),
                pl.BlockSpec((tokens, chunk), lambda j, coords: (0, j)),
                pl.BlockSpec((1, count, rows, chunk), lambda j, coords: (j, 0, 0, 0)),
                pl.BlockSpec((shared_count, block, block), lambda j, coords: (0, 0, 0)),
            ],
            out_specs=[
                pl.BlockSpec((tokens, chunk), lambda j, coords: (0, j)),
                pl.BlockSpec((1, count, rows, chunk), lambda j, coords: (j, 0, 0, 0)),
                pl.BlockSpec((shared_count, block, block), lambda j, coords: (0, 0, 0)),
            ],
            scratch_shapes=[pltpu.VMEM((tokens, chunk), f32)],
        ),
        out_shape=[
            jax.ShapeDtypeStruct((tokens, width), jnp.bfloat16),
            jax.ShapeDtypeStruct((member_chunks, count, rows, chunk), f32),
            jax.ShapeDtypeStruct((shared_count, block, block), f32),
        ],
        compiler_params=pltpu.CompilerParams(
            dimension_semantics=("arbitrary",), vmem_limit_bytes=VMEM_BYTES
        ),
        name="layer",
    )(shared_coords, features, features, cotangent, gathered, shared_blocks)

    shared_rows = shared_term.reshape((ratio, per) + twos + (local, block))
    folded_term = jnp.transpose(
        shared_rows, tuple(2 + b for b in back) + (0, bits + 2, 1, bits + 3)
    ).reshape(count, rows, chunk)

    member_grad, folded_grad = pl.pallas_call(
        functools.partial(scatter_kernel, bits, chunks, chunk),
        out_shape=[
            jax.ShapeDtypeStruct((rows, width), f32),
            jax.ShapeDtypeStruct((rows, chunk), f32),
        ],
        in_specs=[any_space, any_space],
        out_specs=[vmem_space, vmem_space],
        scratch_shapes=[
            pltpu.VMEM((chunks, count, rows, chunk), f32),
            pltpu.VMEM((chunks, count, rows, chunk), jnp.bfloat16),
            pltpu.VMEM((chunks, count, rows, chunk), jnp.bfloat16),
            pltpu.SemaphoreType.DMA((chunks, bits)),
            pltpu.SemaphoreType.DMA((chunks, bits)),
            pltpu.SemaphoreType.DMA((chunks,)),
        ],
        compiler_params=pltpu.CompilerParams(
            collective_id=1, has_side_effects=True, vmem_limit_bytes=VMEM_BYTES
        ),
        name="scatter_gradients",
    )(term, folded_term)
    shared_grad = jnp.transpose(folded_grad.reshape(ratio, local, chunk), (1, 0, 2)).reshape(
        local, shared_count * block
    )
    return (activated, member_grad, shared_grad)


def solution(mesh):
    return jax.shard_map(
        per_device,
        mesh=mesh,
        in_specs=(
            P(("groups", "shard"), None),
            P(("groups", "shard"), None),
            P("shard", None),
            P("shard", None),
            P(),
        ),
        out_specs=(
            P(("groups", "shard"), None),
            P(("groups", "shard"), None),
            P(("groups", "shard"), None),
        ),
        check_vma=False,
    )
```

```python
import functools

import jax
import jax.numpy as jnp
from jax import lax
from jax.experimental import pallas as pl
from jax.experimental.pallas import tpu as pltpu
from jax.sharding import PartitionSpec as P

ROOT_HALF = 0.7071067811865476
INV_ROOT_TWO_PI = 0.3989422804014327
MESH = pl.DeviceIdType.MESH
VMEM_BYTES = 60 * 2**20


def reversed_bits(value, bits):
    out = 0
    for b in range(bits):
        out = out + ((value // 2**b) % 2) * 2 ** (bits - 1 - b)
    return out


def flipped(value, b):
    return value + (1 - 2 * ((value // 2**b) % 2)) * 2**b


def fused_kernel(
    bits, twin, block, shared_count, table_ref, feat_hbm, cot_hbm, member_ref, folded_ref,
    act_hbm, member_out, folded_out,
    feat, cot, grad, act, gathered, acc, out_buf, in_buf, sums,
    own_sem, load_sem, act_sem, gather_send, gather_recv, send, recv,
):
    me = lax.axis_index("shard")
    group = lax.axis_index("groups")
    pos = reversed_bits(me, bits)
    count = 2**bits
    items, _, rows, chunk = gathered.shape
    member_chunks = items - 1
    slots = acc.shape[0]
    per = chunk // block
    ratio = shared_count // per
    local = rows // ratio
    member_width = rows * count
    grid, tokens = feat.shape[:2]
    f32 = jnp.float32
    at_col, at_before, at_last = shared_count, 2 * shared_count, 3 * shared_count

    def peer(b):
        return {"shard": flipped(me, b)}

    across = {"groups": flipped(group, 0)}
    half = group % 2
    stages = []
    for k in range(bits):
        b = bits - 1 - k
        start, size = (pos // 2**k) * 2**k, 2**k
        if b == 1 and twin:
            size //= 2
            stages.append((start + half * size, size, peer(b)))
            there = (flipped(pos, k) // 2**k) * 2**k
            stages.append((there + half * size, size, across))
        else:
            stages.append((start, size, peer(b)))
    ahead = len(stages)

    def gather_copy(g, k):
        start, size, target = stages[k]
        part = gathered.at[g, pl.ds(start, size)]
        return pltpu.make_async_remote_copy(
            src_ref=part,
            dst_ref=part,
            send_sem=gather_send.at[g, k],
            recv_sem=gather_recv.at[g, k],
            device_id=target,
            device_id_type=MESH,
        )

    def span(k):
        size = count // 2 ** (k + 1)
        return count - count // 2**k, size

    def scatter_copy(h, k):
        first, size = span(k)
        return pltpu.make_async_remote_copy(
            src_ref=out_buf.at[h, pl.ds(first, size)],
            dst_ref=in_buf.at[h, pl.ds(first, size)],
            send_sem=send.at[h, k],
            recv_sem=recv.at[h, k],
            device_id=peer(k),
            device_id_type=MESH,
        )

    def columns(j):
        return pl.ds(pl.multiple_of(j * chunk, chunk), chunk)

    def act_copy(j):
        return pltpu.make_async_copy(act.at[j], act_hbm.at[:, columns(j)], act_sem.at[j])

    own = [pltpu.make_async_copy(folded_ref, gathered.at[0, pos], own_sem.at[0])]
    for j in range(member_chunks):
        own.append(
            pltpu.make_async_copy(
                member_ref.at[:, j * chunk : (j + 1) * chunk],
                gathered.at[j + 1, pos],
                own_sem.at[j + 1],
            )
        )
    loads = [pltpu.make_async_copy(cot_hbm, cot, load_sem.at[grid])]
    for i in range(grid):
        loads.append(
            pltpu.make_async_copy(
                feat_hbm.at[:, i * block : (i + 1) * block], feat.at[i], load_sem.at[i]
            )
        )
    for copy in own + loads:
        copy.start()

    barrier = pltpu.get_barrier_semaphore()
    partners = [peer(b) for b in range(bits)] + ([across] if twin else [])
    for target in partners:
        pl.semaphore_signal(barrier, inc=1, device_id=target, device_id_type=MESH)
    pl.semaphore_wait(barrier, len(partners))
    for copy in own:
        copy.wait()

    def shared_inputs(s):
        return feat[table_ref[s]]

    def place(s):
        return s // per, slice((s % per) * block, (s % per + 1) * block)

    def shared_forward():
        @pl.loop(0, count)
        def _(i):
            acc[0, i] = gathered[0, i].astype(f32)

        for q in range(ratio):
            for d in range(count):
                row = q * block + d * local
                acc[1, row // rows, row % rows : row % rows + local] = acc[
                    0, reversed_bits(d, bits), q * local : (q + 1) * local
                ]
        sums[shared_count] = jnp.zeros((tokens, block), f32)
        pieces = block // rows
        for s in range(shared_count):
            q, cols = place(s)
            weights = jnp.concatenate(
                [acc[1, q * pieces + i, :, cols] for i in range(pieces)], axis=0
            ).astype(jnp.bfloat16)
            sums[s] = sums[table_ref[at_before + s]] + jnp.dot(
                shared_inputs(s), weights, preferred_element_type=f32
            )

    def member_step(j):
        across_member = member_width // block
        member = (j * chunk // member_width) * across_member
        inputs = jnp.concatenate([feat[member + i] for i in range(across_member)], axis=1)
        weights = jnp.concatenate(
            [gathered[j + 1, reversed_bits(d, bits)] for d in range(count)], axis=0
        )
        hidden = jnp.dot(inputs, weights, preferred_element_type=f32)
        hidden = hidden + jnp.concatenate(
            [sums[table_ref[at_last + j * per + part]] for part in range(per)], axis=1
        )
        phi = 0.5 * (1.0 + lax.erf(hidden * ROOT_HALF))
        act[j] = (hidden * phi).astype(act.dtype)
        act_copy(j).start()
        slope = phi + hidden * INV_ROOT_TWO_PI * jnp.exp(-0.5 * hidden * hidden)
        new = (cot[:, columns(j)].astype(f32) * slope).astype(jnp.bfloat16)
        for part in range(per):
            grad[j * per + part] = new[:, part * block : (part + 1) * block]
        term = lax.dot_general(
            inputs, new, (((0,), (0,)), ((), ())), preferred_element_type=f32
        )
        for d in range(count):
            acc[j % slots, reversed_bits(d, bits)] = term[d * rows : (d + 1) * rows]

    def shared_step():
        slot = member_chunks % slots
        for s in range(shared_count):
            q, cols = place(s)
            sums[s] = lax.dot_general(
                shared_inputs(s),
                grad[table_ref[at_col + s]],
                (((0,), (0,)), ((), ())),
                preferred_element_type=f32,
            )
            for d in range(count):
                acc[slot, reversed_bits(d, bits), q * local : (q + 1) * local, cols] = sums[
                    s, d * local : (d + 1) * local
                ]

    def scatter_stage(h, k):
        slot = h % slots
        if k > 0:
            scatter_copy(h, k - 1).wait_recv()
            first, size = span(k - 1)
            kept = (pos // size) * size

            @pl.loop(0, size)
            def _(i):
                acc[slot, kept + i] += in_buf[h, first + i].astype(f32)

        if k < bits:
            first, size = span(k)
            leaving = (flipped(pos, bits - 1 - k) // size) * size

            @pl.loop(0, size)
            def _(i):
                out_buf[h, first + i] = acc[slot, leaving + i].astype(out_buf.dtype)

            scatter_copy(h, k).start()
        else:
            @pl.when(h < member_chunks)
            def _():
                member_out[:, columns(h)] = acc[slot, pos]

            @pl.when(h == member_chunks)
            def _():
                folded_out[...] = acc[slot, pos]

    def when_in_range(index, action):
        @pl.when((index >= 0) & (index < items))
        def _():
            action(index)

    @pl.loop(0, items + ahead + 1 + bits)
    def _(wave):
        for k in range(ahead):
            def gather_stage(g, k=k):
                if k > 0:
                    gather_copy(g, k - 1).wait_recv()
                gather_copy(g, k).start()

            when_in_range(wave - k, gather_stage)
        for k in range(1, bits + 1):
            when_in_range(wave - ahead - 1 - k, functools.partial(scatter_stage, k=k))
        when_in_range(wave - ahead, lambda g: gather_copy(g, ahead - 1).wait_recv())

        @pl.when(wave == ahead)
        def _():
            for copy in loads:
                copy.wait()
            shared_forward()

        @pl.when((wave > ahead) & (wave < ahead + items))
        def _():
            member_step(wave - ahead - 1)

        @pl.when(wave == ahead + items)
        def _():
            shared_step()

        when_in_range(wave - ahead - 1, functools.partial(scatter_stage, k=0))

    @pl.loop(0, items)
    def _(g):
        for k in range(ahead):
            gather_copy(g, k).wait_send()
        for k in range(bits):
            scatter_copy(g, k).wait_send()

    @pl.loop(0, member_chunks)
    def _(j):
        act_copy(j).wait()


def per_device(features, cotangent, member_weight, shared_weight, shared_coords):
    count = lax.axis_size("shard")
    bits = count.bit_length() - 1
    twin = lax.axis_size("groups") % 2 == 0 and bits >= 3
    ahead = bits + int(twin)
    tokens, width = features.shape
    rows = member_weight.shape[0]
    local = shared_weight.shape[0]
    block = local * count
    shared_count = shared_coords.shape[0]
    ratio = rows // local
    chunk = shared_count * block // ratio
    member_chunks = width // chunk
    items = member_chunks + 1
    f32, bf16 = jnp.float32, jnp.bfloat16
    any_space = pl.BlockSpec(memory_space=pl.ANY)
    vmem_space = pl.BlockSpec(memory_space=pltpu.VMEM)

    folded = jnp.transpose(shared_weight.reshape(local, ratio, chunk), (1, 0, 2)).reshape(rows, chunk)
    cols = shared_coords[:, 1]
    order = jnp.arange(shared_count, dtype=jnp.int32)

    def last_with(column, upto):
        hit = (cols[None, :] == column[:, None]) & (order[None, :] < upto[:, None])
        found = jnp.max(jnp.where(hit, order[None, :], -1), axis=1)
        return jnp.where(found < 0, shared_count, found)

    grid = jnp.arange(width // block, dtype=jnp.int32)
    table = jnp.concatenate(
        [
            shared_coords[:, 0],
            cols,
            last_with(
                jnp.concatenate([cols, grid]),
                jnp.concatenate([order, jnp.full_like(grid, shared_count)]),
            ),
        ]
    )
    activated, member_grad, folded_grad = pl.pallas_call(
        functools.partial(fused_kernel, bits, twin, block, shared_count),
        out_shape=[
            jax.ShapeDtypeStruct((tokens, width), bf16),
            jax.ShapeDtypeStruct((rows, width), f32),
            jax.ShapeDtypeStruct((rows, chunk), f32),
        ],
        in_specs=[pl.BlockSpec(memory_space=pltpu.SMEM)] + [any_space] * 4,
        out_specs=[any_space, vmem_space, vmem_space],
        scratch_shapes=[
            pltpu.VMEM((width // block, tokens, block), bf16),
            pltpu.VMEM((tokens, width), bf16),
            pltpu.VMEM((width // block, tokens, block), bf16),
            pltpu.VMEM((member_chunks, tokens, chunk), bf16),
            pltpu.VMEM((items, count, rows, chunk), bf16),
            pltpu.VMEM((bits + 2, count, rows, chunk), f32),
            pltpu.VMEM((items, count, rows, chunk), bf16),
            pltpu.VMEM((items, count, rows, chunk), bf16),
            pltpu.VMEM((shared_count + 1, max(tokens, block), block), f32),
            pltpu.SemaphoreType.DMA((items,)),
            pltpu.SemaphoreType.DMA((width // block + 1,)),
            pltpu.SemaphoreType.DMA((member_chunks,)),
            pltpu.SemaphoreType.DMA((items, ahead)),
            pltpu.SemaphoreType.DMA((items, ahead)),
            pltpu.SemaphoreType.DMA((items, bits)),
            pltpu.SemaphoreType.DMA((items, bits)),
        ],
        compiler_params=pltpu.CompilerParams(
            collective_id=0, has_side_effects=True, vmem_limit_bytes=VMEM_BYTES
        ),
        name="fused_layer",
    )(table, features, cotangent, member_weight, folded)
    shared_grad = jnp.transpose(folded_grad.reshape(ratio, local, chunk), (1, 0, 2)).reshape(
        local, shared_count * block
    )
    return (activated, member_grad, shared_grad)


def solution(mesh):
    return jax.shard_map(
        per_device,
        mesh=mesh,
        in_specs=(
            P(("groups", "shard"), None),
            P(("groups", "shard"), None),
            P("shard", None),
            P("shard", None),
            P(),
        ),
        out_specs=(
            P(("groups", "shard"), None),
            P(("groups", "shard"), None),
            P(("groups", "shard"), None),
        ),
        check_vma=False,
    )
```

```python
import functools

import jax
import jax.numpy as jnp
from jax import lax
from jax.experimental import pallas as pl
from jax.experimental.pallas import tpu as pltpu
from jax.sharding import PartitionSpec as P

ROOT_HALF = 0.7071067811865476
INV_ROOT_TWO_PI = 0.3989422804014327
MESH = pl.DeviceIdType.MESH
CHUNK_BLOCKS = 1
VMEM_BYTES = 60 * 2**20


def reversed_bits(value, bits):
    out = 0
    for b in range(bits):
        out = out + ((value // 2**b) % 2) * 2 ** (bits - 1 - b)
    return out


def flipped(value, b):
    return value + (1 - 2 * ((value // 2**b) % 2)) * 2**b


def fused_kernel(
    bits, twin, block, shared_items, coords_ref, feat_hbm, cot_hbm, member_ref, folded_ref,
    act_hbm, member_out, folded_out,
    feat, cot, grad, act, gathered, acc, out_buf, in_buf, sums,
    own_sem, load_sem, act_sem, gather_send, gather_recv, send, recv,
):
    me = lax.axis_index("shard")
    group = lax.axis_index("groups")
    pos = reversed_bits(me, bits)
    count = 2**bits
    items, _, rows, chunk = gathered.shape
    member_chunks = items - shared_items
    shared_count = coords_ref.shape[0]
    slots = acc.shape[0]
    per = chunk // block
    folded_blocks = shared_items * per
    ratio = shared_count // folded_blocks
    local = rows // ratio
    member_width = rows * count
    grid, tokens = feat.shape[:2]
    f32 = jnp.float32
    arrival = [q * folded_blocks + e for e in range(folded_blocks) for q in range(ratio)]

    def last_of(column, positions):
        found = jnp.int32(0)
        for t in positions:
            apart = coords_ref[arrival[t], 1] - column
            found = jnp.maximum(found, (1 - jnp.minimum(apart * apart, 1)) * (t + 1))
        return found

    def peer(b):
        return {"shard": flipped(me, b)}

    across = {"groups": flipped(group, 0)}
    half = group % 2
    stages = []
    for k in range(bits):
        b = bits - 1 - k
        start, size = (pos // 2**k) * 2**k, 2**k
        if b == 1 and twin:
            size //= 2
            stages.append((start + half * size, size, peer(b)))
            there = (flipped(pos, k) // 2**k) * 2**k
            stages.append((there + half * size, size, across))
        else:
            stages.append((start, size, peer(b)))
    ahead = len(stages)

    def gather_copy(g, k):
        start, size, target = stages[k]
        part = gathered.at[g, pl.ds(start, size)]
        return pltpu.make_async_remote_copy(
            src_ref=part,
            dst_ref=part,
            send_sem=gather_send.at[g, k],
            recv_sem=gather_recv.at[g, k],
            device_id=target,
            device_id_type=MESH,
        )

    def span(k):
        size = count // 2 ** (k + 1)
        return count - count // 2**k, size

    def scatter_copy(h, k):
        first, size = span(k)
        return pltpu.make_async_remote_copy(
            src_ref=out_buf.at[h, pl.ds(first, size)],
            dst_ref=in_buf.at[h, pl.ds(first, size)],
            send_sem=send.at[h, k],
            recv_sem=recv.at[h, k],
            device_id=peer(k),
            device_id_type=MESH,
        )

    def columns(j):
        return pl.ds(pl.multiple_of(j * chunk, chunk), chunk)

    def act_copy(j):
        return pltpu.make_async_copy(act.at[j], act_hbm.at[:, columns(j)], act_sem.at[j])

    own = []
    for g in range(items):
        ref, j = (folded_ref, g) if g < shared_items else (member_ref, g - shared_items)
        own.append(
            pltpu.make_async_copy(
                ref.at[:, j * chunk : (j + 1) * chunk], gathered.at[g, pos], own_sem.at[g]
            )
        )
    loads = [pltpu.make_async_copy(cot_hbm, cot, load_sem.at[grid])]
    for i in range(grid):
        loads.append(
            pltpu.make_async_copy(
                feat_hbm.at[:, i * block : (i + 1) * block], feat.at[i], load_sem.at[i]
            )
        )
    for copy in own + loads:
        copy.start()

    barrier = pltpu.get_barrier_semaphore()
    partners = [peer(b) for b in range(bits)] + ([across] if twin else [])
    for target in partners:
        pl.semaphore_signal(barrier, inc=1, device_id=target, device_id_type=MESH)
    pl.semaphore_wait(barrier, len(partners))
    for copy in own:
        copy.wait()

    def shared_inputs(s):
        return feat[coords_ref[s, 0]]

    def place(s):
        q, e = s // folded_blocks, s % folded_blocks
        return q, e // per, slice((e % per) * block, (e % per + 1) * block)

    def shared_forward():
        sums[0] = jnp.zeros((tokens, block), f32)
        pieces = block // rows
        for t, s in enumerate(arrival):
            q, item, cols = place(s)
            if t % (ratio * per) == 0:
                @pl.loop(0, count)
                def _(i):
                    acc[0, i] = gathered[item, i].astype(f32)

                for r in range(ratio):
                    for d in range(count):
                        row = r * block + d * local
                        acc[1, row // rows, row % rows : row % rows + local] = acc[
                            0, reversed_bits(d, bits), r * local : (r + 1) * local
                        ]
            weights = jnp.concatenate(
                [acc[1, q * pieces + i, :, cols] for i in range(pieces)], axis=0
            ).astype(jnp.bfloat16)
            sums[t + 1] = sums[last_of(coords_ref[s, 1], range(t))] + jnp.dot(
                shared_inputs(s), weights, preferred_element_type=f32
            )

    def member_step(j):
        across_member = member_width // block
        member = (j * chunk // member_width) * across_member
        inputs = jnp.concatenate([feat[member + i] for i in range(across_member)], axis=1)
        weights = jnp.concatenate(
            [gathered[j + shared_items, reversed_bits(d, bits)] for d in range(count)], axis=0
        )
        hidden = jnp.dot(inputs, weights, preferred_element_type=f32)
        hidden = hidden + jnp.concatenate(
            [sums[last_of(j * per + part, range(shared_count))] for part in range(per)], axis=1
        )
        phi = 0.5 * (1.0 + lax.erf(hidden * ROOT_HALF))
        act[j] = (hidden * phi).astype(act.dtype)
        act_copy(j).start()
        slope = phi + hidden * INV_ROOT_TWO_PI * jnp.exp(-0.5 * hidden * hidden)
        new = (cot[:, columns(j)].astype(f32) * slope).astype(jnp.bfloat16)
        for part in range(per):
            grad[j * per + part] = new[:, part * block : (part + 1) * block]
        term = lax.dot_general(
            inputs, new, (((0,), (0,)), ((), ())), preferred_element_type=f32
        )
        for d in range(count):
            acc[j % slots, reversed_bits(d, bits)] = term[d * rows : (d + 1) * rows]

    def shared_step(item):
        slot = (member_chunks + item) % slots
        for s in range(shared_count):
            q, its_item, cols = place(s)
            if its_item != item:
                continue
            sums[s] = lax.dot_general(
                shared_inputs(s),
                grad[coords_ref[s, 1]],
                (((0,), (0,)), ((), ())),
                preferred_element_type=f32,
            )
            for d in range(count):
                acc[slot, reversed_bits(d, bits), q * local : (q + 1) * local, cols] = sums[
                    s, d * local : (d + 1) * local
                ]

    def scatter_stage(h, k):
        slot = h % slots
        if k > 0:
            scatter_copy(h, k - 1).wait_recv()
            first, size = span(k - 1)
            kept = (pos // size) * size

            @pl.loop(0, size)
            def _(i):
                acc[slot, kept + i] += in_buf[h, first + i].astype(f32)

        if k < bits:
            first, size = span(k)
            leaving = (flipped(pos, bits - 1 - k) // size) * size

            @pl.loop(0, size)
            def _(i):
                out_buf[h, first + i] = acc[slot, leaving + i].astype(out_buf.dtype)

            scatter_copy(h, k).start()
        else:
            @pl.when(h < member_chunks)
            def _():
                member_out[:, columns(h)] = acc[slot, pos]

            @pl.when(h >= member_chunks)
            def _():
                folded_out[:, columns(h - member_chunks)] = acc[slot, pos]

    def when_in_range(index, action):
        @pl.when((index >= 0) & (index < items))
        def _():
            action(index)

    base = ahead + shared_items

    @pl.loop(0, base + items + bits)
    def _(wave):
        for k in range(ahead):
            def gather_stage(g, k=k):
                if k > 0:
                    gather_copy(g, k - 1).wait_recv()
                gather_copy(g, k).start()

            when_in_range(wave - k, gather_stage)
        for k in range(1, bits + 1):
            when_in_range(wave - base - k, functools.partial(scatter_stage, k=k))
        when_in_range(wave - ahead, lambda g: gather_copy(g, ahead - 1).wait_recv())

        @pl.when(wave == base - 1)
        def _():
            for copy in loads:
                copy.wait()
            shared_forward()

        @pl.when((wave >= base) & (wave < base + member_chunks))
        def _():
            member_step(wave - base)

        for item in range(shared_items):
            @pl.when(wave == base + member_chunks + item)
            def _():
                shared_step(item)

        when_in_range(wave - base, functools.partial(scatter_stage, k=0))

    @pl.loop(0, items)
    def _(g):
        for k in range(ahead):
            gather_copy(g, k).wait_send()
        for k in range(bits):
            scatter_copy(g, k).wait_send()

    @pl.loop(0, member_chunks)
    def _(j):
        act_copy(j).wait()


def per_device(features, cotangent, member_weight, shared_weight, shared_coords):
    count = lax.axis_size("shard")
    bits = count.bit_length() - 1
    twin = lax.axis_size("groups") % 2 == 0 and bits >= 3
    ahead = bits + int(twin)
    tokens, width = features.shape
    rows = member_weight.shape[0]
    local = shared_weight.shape[0]
    block = local * count
    shared_count = shared_coords.shape[0]
    ratio = rows // local
    folded_width = shared_count * block // ratio
    chunk = CHUNK_BLOCKS * block
    member_chunks = width // chunk
    shared_items = folded_width // chunk
    items = member_chunks + shared_items
    f32, bf16 = jnp.float32, jnp.bfloat16
    any_space = pl.BlockSpec(memory_space=pl.ANY)
    vmem_space = pl.BlockSpec(memory_space=pltpu.VMEM)

    folded = jnp.transpose(shared_weight.reshape(local, ratio, folded_width), (1, 0, 2)).reshape(
        rows, folded_width
    )
    activated, member_grad, folded_grad = pl.pallas_call(
        functools.partial(fused_kernel, bits, twin, block, shared_items),
        out_shape=[
            jax.ShapeDtypeStruct((tokens, width), bf16),
            jax.ShapeDtypeStruct((rows, width), f32),
            jax.ShapeDtypeStruct((rows, folded_width), f32),
        ],
        in_specs=[pl.BlockSpec(memory_space=pltpu.SMEM)] + [any_space] * 4,
        out_specs=[any_space, vmem_space, vmem_space],
        scratch_shapes=[
            pltpu.VMEM((width // block, tokens, block), bf16),
            pltpu.VMEM((tokens, width), bf16),
            pltpu.VMEM((width // block, tokens, block), bf16),
            pltpu.VMEM((member_chunks, tokens, chunk), bf16),
            pltpu.VMEM((items, count, rows, chunk), bf16),
            pltpu.VMEM((bits + 2, count, rows, chunk), f32),
            pltpu.VMEM((items, count, rows, chunk), bf16),
            pltpu.VMEM((items, count, rows, chunk), bf16),
            pltpu.VMEM((shared_count + 1, max(tokens, block), block), f32),
            pltpu.SemaphoreType.DMA((items,)),
            pltpu.SemaphoreType.DMA((width // block + 1,)),
            pltpu.SemaphoreType.DMA((member_chunks,)),
            pltpu.SemaphoreType.DMA((items, ahead)),
            pltpu.SemaphoreType.DMA((items, ahead)),
            pltpu.SemaphoreType.DMA((items, bits)),
            pltpu.SemaphoreType.DMA((items, bits)),
        ],
        compiler_params=pltpu.CompilerParams(
            collective_id=0, has_side_effects=True, vmem_limit_bytes=VMEM_BYTES
        ),
        name="fused_layer",
    )(shared_coords, features, cotangent, member_weight, folded)
    shared_grad = jnp.transpose(folded_grad.reshape(ratio, local, folded_width), (1, 0, 2)).reshape(
        local, shared_count * block
    )
    return (activated, member_grad, shared_grad)


def solution(mesh):
    return jax.shard_map(
        per_device,
        mesh=mesh,
        in_specs=(
            P(("groups", "shard"), None),
            P(("groups", "shard"), None),
            P("shard", None),
            P("shard", None),
            P(),
        ),
        out_specs=(
            P(("groups", "shard"), None),
            P(("groups", "shard"), None),
            P(("groups", "shard"), None),
        ),
        check_vma=False,
    )
```

```python
import functools

import jax
import jax.numpy as jnp
from jax import lax
from jax.experimental import pallas as pl
from jax.experimental.pallas import tpu as pltpu
from jax.sharding import PartitionSpec as P

ROOT_HALF = 0.7071067811865476
INV_ROOT_TWO_PI = 0.3989422804014327
MESH = pl.DeviceIdType.MESH
CHUNK_BLOCKS = 1
GATHER_LAG = 2
SCATTER_LAG = 2
VMEM_BYTES = 60 * 2**20


def reversed_bits(value, bits):
    out = 0
    for b in range(bits):
        out = out + ((value // 2**b) % 2) * 2 ** (bits - 1 - b)
    return out


def flipped(value, b):
    return value + (1 - 2 * ((value // 2**b) % 2)) * 2**b


def fused_kernel(
    bits, twin, block, shared_items, coords_ref, feat_hbm, cot_hbm, member_ref, folded_ref,
    act_hbm, member_out, folded_out,
    feat, cot, grad, act, gathered, acc, out_buf, in_buf, sums,
    own_sem, load_sem, act_sem, gather_send, gather_recv, send, recv,
):
    me = lax.axis_index("shard")
    group = lax.axis_index("groups")
    pos = reversed_bits(me, bits)
    count = 2**bits
    items, _, rows, chunk = gathered.shape
    member_chunks = items - shared_items
    shared_count = coords_ref.shape[0]
    slots = acc.shape[0]
    per = chunk // block
    folded_blocks = shared_items * per
    ratio = shared_count // folded_blocks
    local = rows // ratio
    member_width = rows * count
    grid, tokens = feat.shape[:2]
    f32 = jnp.float32
    arrival = [q * folded_blocks + e for e in range(folded_blocks) for q in range(ratio)]

    def last_of(column, positions):
        found = jnp.int32(0)
        for t in positions:
            apart = coords_ref[arrival[t], 1] - column
            found = jnp.maximum(found, (1 - jnp.minimum(apart * apart, 1)) * (t + 1))
        return found

    def peer(b):
        return {"shard": flipped(me, b)}

    across = {"groups": flipped(group, 0)}
    half = group % 2
    stages = []
    for k in range(bits):
        b = bits - 1 - k
        start, size = (pos // 2**k) * 2**k, 2**k
        if b == 1 and twin:
            size //= 2
            stages.append((start + half * size, size, peer(b)))
            there = (flipped(pos, k) // 2**k) * 2**k
            stages.append((there + half * size, size, across))
        else:
            stages.append((start, size, peer(b)))
    ahead = len(stages)

    def gather_copy(g, k):
        start, size, target = stages[k]
        part = gathered.at[g, pl.ds(start, size)]
        return pltpu.make_async_remote_copy(
            src_ref=part,
            dst_ref=part,
            send_sem=gather_send.at[g, k],
            recv_sem=gather_recv.at[g, k],
            device_id=target,
            device_id_type=MESH,
        )

    def span(k):
        size = count // 2 ** (k + 1)
        return count - count // 2**k, size

    def scatter_copy(h, k):
        first, size = span(k)
        return pltpu.make_async_remote_copy(
            src_ref=out_buf.at[h, pl.ds(first, size)],
            dst_ref=in_buf.at[h, pl.ds(first, size)],
            send_sem=send.at[h, k],
            recv_sem=recv.at[h, k],
            device_id=peer(k),
            device_id_type=MESH,
        )

    def columns(j):
        return pl.ds(pl.multiple_of(j * chunk, chunk), chunk)

    def act_copy(j):
        return pltpu.make_async_copy(act.at[j], act_hbm.at[:, columns(j)], act_sem.at[j])

    own = []
    for g in range(items):
        ref, j = (folded_ref, g) if g < shared_items else (member_ref, g - shared_items)
        own.append(
            pltpu.make_async_copy(
                ref.at[:, j * chunk : (j + 1) * chunk], gathered.at[g, pos], own_sem.at[g]
            )
        )
    loads = [pltpu.make_async_copy(cot_hbm, cot, load_sem.at[grid])]
    for i in range(grid):
        loads.append(
            pltpu.make_async_copy(
                feat_hbm.at[:, i * block : (i + 1) * block], feat.at[i], load_sem.at[i]
            )
        )
    for copy in own + loads:
        copy.start()

    barrier = pltpu.get_barrier_semaphore()
    partners = [peer(b) for b in range(bits)] + ([across] if twin else [])
    for target in partners:
        pl.semaphore_signal(barrier, inc=1, device_id=target, device_id_type=MESH)
    pl.semaphore_wait(barrier, len(partners))
    for copy in own:
        copy.wait()

    def shared_inputs(s):
        return feat[coords_ref[s, 0]]

    def place(s):
        q, e = s // folded_blocks, s % folded_blocks
        return q, e // per, slice((e % per) * block, (e % per + 1) * block)

    def shared_forward():
        sums[0] = jnp.zeros((tokens, block), f32)
        pieces = block // rows
        for t, s in enumerate(arrival):
            q, item, cols = place(s)
            if t % (ratio * per) == 0:
                @pl.loop(0, count)
                def _(i):
                    acc[0, i] = gathered[item, i].astype(f32)

                for r in range(ratio):
                    for d in range(count):
                        row = r * block + d * local
                        acc[1, row // rows, row % rows : row % rows + local] = acc[
                            0, reversed_bits(d, bits), r * local : (r + 1) * local
                        ]
            weights = jnp.concatenate(
                [acc[1, q * pieces + i, :, cols] for i in range(pieces)], axis=0
            ).astype(jnp.bfloat16)
            sums[t + 1] = sums[last_of(coords_ref[s, 1], range(t))] + jnp.dot(
                shared_inputs(s), weights, preferred_element_type=f32
            )

    def member_step(j):
        across_member = member_width // block
        member = (j * chunk // member_width) * across_member
        inputs = jnp.concatenate([feat[member + i] for i in range(across_member)], axis=1)
        weights = jnp.concatenate(
            [gathered[j + shared_items, reversed_bits(d, bits)] for d in range(count)], axis=0
        )
        hidden = jnp.dot(inputs, weights, preferred_element_type=f32)
        hidden = hidden + jnp.concatenate(
            [sums[last_of(j * per + part, range(shared_count))] for part in range(per)], axis=1
        )
        phi = 0.5 * (1.0 + lax.erf(hidden * ROOT_HALF))
        act[j] = (hidden * phi).astype(act.dtype)
        act_copy(j).start()
        slope = phi + hidden * INV_ROOT_TWO_PI * jnp.exp(-0.5 * hidden * hidden)
        new = (cot[:, columns(j)].astype(f32) * slope).astype(jnp.bfloat16)
        for part in range(per):
            grad[j * per + part] = new[:, part * block : (part + 1) * block]
        term = lax.dot_general(
            inputs, new, (((0,), (0,)), ((), ())), preferred_element_type=f32
        )
        for d in range(count):
            acc[j % slots, reversed_bits(d, bits)] = term[d * rows : (d + 1) * rows]

    def shared_step(item):
        slot = (member_chunks + item) % slots
        for s in range(shared_count):
            q, its_item, cols = place(s)
            if its_item != item:
                continue
            sums[s] = lax.dot_general(
                shared_inputs(s),
                grad[coords_ref[s, 1]],
                (((0,), (0,)), ((), ())),
                preferred_element_type=f32,
            )
            for d in range(count):
                acc[slot, reversed_bits(d, bits), q * local : (q + 1) * local, cols] = sums[
                    s, d * local : (d + 1) * local
                ]

    def scatter_stage(h, k):
        slot = h % slots
        if k > 0:
            scatter_copy(h, k - 1).wait_recv()
            first, size = span(k - 1)
            kept = (pos // size) * size

            @pl.loop(0, size)
            def _(i):
                acc[slot, kept + i] += in_buf[h, first + i].astype(f32)

        if k < bits:
            first, size = span(k)
            leaving = (flipped(pos, bits - 1 - k) // size) * size

            @pl.loop(0, size)
            def _(i):
                out_buf[h, first + i] = acc[slot, leaving + i].astype(out_buf.dtype)

            scatter_copy(h, k).start()
        else:
            @pl.when(h < member_chunks)
            def _():
                member_out[:, columns(h)] = acc[slot, pos]

            @pl.when(h >= member_chunks)
            def _():
                folded_out[:, columns(h - member_chunks)] = acc[slot, pos]

    def when_in_range(index, action):
        @pl.when((index >= 0) & (index < items))
        def _():
            action(index)

    base = ahead * GATHER_LAG + shared_items

    @pl.loop(0, base + items + bits * SCATTER_LAG)
    def _(wave):
        for k in range(ahead):
            def gather_stage(g, k=k):
                if k > 0:
                    gather_copy(g, k - 1).wait_recv()
                gather_copy(g, k).start()

            when_in_range(wave - k * GATHER_LAG, gather_stage)
        for k in range(1, bits + 1):
            when_in_range(wave - base - k * SCATTER_LAG, functools.partial(scatter_stage, k=k))
        when_in_range(
            wave - ahead * GATHER_LAG, lambda g: gather_copy(g, ahead - 1).wait_recv()
        )

        @pl.when(wave == base - 1)
        def _():
            for copy in loads:
                copy.wait()
            shared_forward()

        @pl.when((wave >= base) & (wave < base + member_chunks))
        def _():
            member_step(wave - base)

        for item in range(shared_items):
            @pl.when(wave == base + member_chunks + item)
            def _():
                shared_step(item)

        when_in_range(wave - base, functools.partial(scatter_stage, k=0))

    @pl.loop(0, items)
    def _(g):
        for k in range(ahead):
            gather_copy(g, k).wait_send()
        for k in range(bits):
            scatter_copy(g, k).wait_send()

    @pl.loop(0, member_chunks)
    def _(j):
        act_copy(j).wait()


def per_device(features, cotangent, member_weight, shared_weight, shared_coords):
    count = lax.axis_size("shard")
    bits = count.bit_length() - 1
    twin = lax.axis_size("groups") % 2 == 0 and bits >= 3
    ahead = bits + int(twin)
    tokens, width = features.shape
    rows = member_weight.shape[0]
    local = shared_weight.shape[0]
    block = local * count
    shared_count = shared_coords.shape[0]
    ratio = rows // local
    folded_width = shared_count * block // ratio
    chunk = CHUNK_BLOCKS * block
    member_chunks = width // chunk
    shared_items = folded_width // chunk
    items = member_chunks + shared_items
    f32, bf16 = jnp.float32, jnp.bfloat16
    any_space = pl.BlockSpec(memory_space=pl.ANY)
    vmem_space = pl.BlockSpec(memory_space=pltpu.VMEM)

    folded = jnp.transpose(shared_weight.reshape(local, ratio, folded_width), (1, 0, 2)).reshape(
        rows, folded_width
    )
    activated, member_grad, folded_grad = pl.pallas_call(
        functools.partial(fused_kernel, bits, twin, block, shared_items),
        out_shape=[
            jax.ShapeDtypeStruct((tokens, width), bf16),
            jax.ShapeDtypeStruct((rows, width), f32),
            jax.ShapeDtypeStruct((rows, folded_width), f32),
        ],
        in_specs=[pl.BlockSpec(memory_space=pltpu.SMEM)] + [any_space] * 4,
        out_specs=[any_space, vmem_space, vmem_space],
        scratch_shapes=[
            pltpu.VMEM((width // block, tokens, block), bf16),
            pltpu.VMEM((tokens, width), bf16),
            pltpu.VMEM((width // block, tokens, block), bf16),
            pltpu.VMEM((member_chunks, tokens, chunk), bf16),
            pltpu.VMEM((items, count, rows, chunk), bf16),
            pltpu.VMEM((bits * SCATTER_LAG + 2, count, rows, chunk), f32),
            pltpu.VMEM((items, count, rows, chunk), bf16),
            pltpu.VMEM((items, count, rows, chunk), bf16),
            pltpu.VMEM((shared_count + 1, max(tokens, block), block), f32),
            pltpu.SemaphoreType.DMA((items,)),
            pltpu.SemaphoreType.DMA((width // block + 1,)),
            pltpu.SemaphoreType.DMA((member_chunks,)),
            pltpu.SemaphoreType.DMA((items, ahead)),
            pltpu.SemaphoreType.DMA((items, ahead)),
            pltpu.SemaphoreType.DMA((items, bits)),
            pltpu.SemaphoreType.DMA((items, bits)),
        ],
        compiler_params=pltpu.CompilerParams(
            collective_id=0, has_side_effects=True, vmem_limit_bytes=VMEM_BYTES
        ),
        name="fused_layer",
    )(shared_coords, features, cotangent, member_weight, folded)
    shared_grad = jnp.transpose(folded_grad.reshape(ratio, local, folded_width), (1, 0, 2)).reshape(
        local, shared_count * block
    )
    return (activated, member_grad, shared_grad)


def solution(mesh):
    return jax.shard_map(
        per_device,
        mesh=mesh,
        in_specs=(
            P(("groups", "shard"), None),
            P(("groups", "shard"), None),
            P("shard", None),
            P("shard", None),
            P(),
        ),
        out_specs=(
            P(("groups", "shard"), None),
            P(("groups", "shard"), None),
            P(("groups", "shard"), None),
        ),
        check_vma=False,
    )
```
